512 devices in a mesh: fsdp: 64 (over x, z), tensor: 8 (over y, core).
Axes of the slice: x: 4, y: 4, z: 16, core: 2. Of those that a mesh axis runs over, the one named last changes fastest.
Arguments:
- gate_pre: bfloat16 [12288, 14336], P(('fsdp', 'tensor')), may hold values from -6 to 6
- up_pre: bfloat16 [12288, 14336], P(('fsdp', 'tensor')), may hold values from -6 to 6
- cotangent: bfloat16 [12288, 4096], P('fsdp'), may hold values from -6 to 6
- w_slots: bfloat16 [8, 192, 128, 128], P('tensor', 'fsdp'), may hold values from -0.15625 to 0.15625
- slot_ids: int32 [8, 192], P('tensor'), may hold values from -1 to 447, as said below
Outputs:
- d_gate: bfloat16 [12288, 14336], P(('fsdp', 'tensor'))
- d_up: bfloat16 [12288, 14336], P(('fsdp', 'tensor'))
- w_grad: float32 [8, 192, 128, 128], P('tensor', 'fsdp')
The draws below stay inside these ranges and needn't reach their ends.
Inputs may be any that keep to these rules, and one draw needn't show every extreme that they name: `slot_ids`: in row t, slots s * 3 to s * 3 + 2 list the kept blocks owned by fsdp index s in tensor slice t as local row block * 32 + column block, filling the first slots and -1 in the rest; every owner has 2 or 3 kept blocks, some owner of every row exactly 3 and some exactly 2; no block id appears twice in a row.
All inputs are finite; a program needn't handle non-finite values.
Results may differ from the reference program's by a relative error of at most 0.0085.
Values may be sent and summed in bfloat16 or wider, within the bound.
No kernel may reach another device: no remote copies, remote signals or barrier semaphores. Data moves between devices by JAX's collectives and lax.ppermute only.
A program may use at most 128 MiB of HBM per device.

```python
import math
import jax
import jax.numpy as jnp
from jax import lax

D = 4096
FF = 14336
BLOCK = 128
CAP = 3
TOK_DEV = 192
TOKENS = 12288
SLOTS = 192
N_FSDP = 64
N_TENSOR = 8


def draw_slot_ids(key, part):
    block_total = FF // (N_TENSOR * BLOCK) * (D // BLOCK)
    key_list = jax.random.split(jax.random.fold_in(key, 11), N_TENSOR)

    def one_slice(slice_key):
        key_a, key_b, key_c, key_d = jax.random.split(slice_key, 4)
        shuffled = jax.random.permutation(key_a, block_total - 1)[:CAP * N_FSDP].astype(jnp.int32)
        shortfall = (jax.random.randint(key_b, (N_FSDP,), 0, 4) == 0).astype(jnp.int32)
        full_owner = jax.random.randint(key_c, (), 0, N_FSDP)
        short_owner = (full_owner + 1 + jax.random.randint(key_d, (), 0, N_FSDP - 1)) % N_FSDP
        owner_index = jnp.arange(N_FSDP)
        shortfall = jnp.where(owner_index == full_owner, 0, jnp.where(owner_index == short_owner, 1, shortfall))
        slot_index = jnp.arange(CAP * N_FSDP)
        shuffled = jnp.where(slot_index == full_owner * CAP, block_total - 1, shuffled).astype(jnp.int32)
        kept_count = CAP - shortfall
        keep_slot = jnp.arange(CAP)[None, :] < kept_count[:, None]
        return jnp.where(keep_slot, shuffled.reshape(N_FSDP, CAP), -1).reshape(-1)
    return jax.vmap(one_slice)(key_list).astype(jnp.int32)


def block_levels(rng, extent, pieces, smallest, top_value):
    factor_of, own = 1.0, jax.random.fold_in(rng, 6)
    for axis_at, parts in pieces:
        draws = jnp.exp(jax.random.uniform(jax.random.fold_in(own, axis_at), (parts,), jnp.float32, smallest / len(pieces), top_value / len(pieces)))
        factor_of = factor_of * jnp.repeat(draws, extent[axis_at] // parts).reshape([-1 if axis == axis_at else 1 for axis in range(len(extent))])
    return factor_of


def noise(key, shape, deviation, most, shards=(), kind=jnp.bfloat16):
    drawn = jax.random.normal(key, shape, jnp.float32) * deviation
    if len(shards) > 0:
        drawn = block_levels(key, shape, shards, -0.22, 0.18) * drawn
    return jnp.clip(drawn, min=-most, max=most).astype(kind)


def setup_inputs(seed: int = 0) -> dict:
    keys = jax.random.split(jax.random.key(seed), 6)
    gate_pre = noise(keys[0], (TOKENS, FF), 1.0, 6.0, ((0, 512),))
    up_pre = noise(keys[1], (TOKENS, FF), 1.0, 6.0, ((0, 512),))
    cotangent = noise(keys[2], (TOKENS, D), 1.0, 6.0, ((0, 64),))
    w_slots = noise(keys[3], (N_TENSOR, SLOTS, BLOCK, BLOCK), (D * 2 // 5) ** -0.5, 0.15625, ((0, 8), (1, 64)))
    slot_ids = draw_slot_ids(jax.random.fold_in(keys[5], 71), 0)
    return dict(gate_pre=gate_pre, up_pre=up_pre, cotangent=cotangent, w_slots=w_slots, slot_ids=slot_ids)


def reference(gate_pre, up_pre, cotangent, w_slots, slot_ids):
    n_slice = N_TENSOR
    ff_dev = FF // N_TENSOR
    row_count = ff_dev // BLOCK
    col_count = D // BLOCK
    gate_f = gate_pre.astype(jnp.float32)
    up_f = up_pre.astype(jnp.float32)
    gate_sig = jax.nn.sigmoid(gate_f)
    hidden = (gate_f * gate_sig * up_f).astype(jnp.bfloat16)
    usable = slot_ids >= 0
    safe_ids = jnp.maximum(slot_ids, 0)
    row_index = jnp.where(usable, safe_ids // col_count, row_count).astype(jnp.int32)
    col_index = (safe_ids % col_count).astype(jnp.int32)
    row_clip = jnp.minimum(row_index, row_count - 1)
    slice_index = jnp.broadcast_to(jnp.arange(n_slice, dtype=jnp.int32)[:, None], slot_ids.shape)
    flat_rows = (slice_index * row_count + row_clip).reshape(-1)
    onehot = (row_index[:, :, None] == jnp.arange(row_count, dtype=jnp.int32)[None, None, :]).astype(jnp.float32)
    weight_f = w_slots.astype(jnp.float32)
    grad_scale = 1.0 / math.sqrt(TOKENS)
    usable_f = usable.astype(jnp.float32)
    hidden_groups = hidden.reshape(N_FSDP, TOK_DEV, n_slice * row_count, BLOCK)
    cot_groups = cotangent.reshape(N_FSDP, TOK_DEV, col_count, BLOCK)

    def advance(running, packed_item):
        hidden_g, cot_g = packed_item
        dy_picked = jnp.take(cot_g, col_index.reshape(-1), axis=1).reshape(TOK_DEV, n_slice, SLOTS, BLOCK).astype(jnp.float32)
        h_picked = jnp.take(hidden_g, flat_rows, axis=1).reshape(TOK_DEV, n_slice, SLOTS, BLOCK).astype(jnp.float32)
        contrib = jnp.einsum('ktsb,tsab->ktsa', dy_picked, weight_f, precision=lax.Precision.HIGHEST)
        dh_blocks = jnp.einsum('ktsa,tsr->ktra', contrib, onehot, precision=lax.Precision.HIGHEST)
        partial_value = jnp.einsum('ktsa,ktsb->tsab', h_picked, dy_picked, precision=lax.Precision.HIGHEST)
        partial_value = (partial_value * (grad_scale * usable_f)[:, :, None, None]).astype(jnp.bfloat16)
        return (running + partial_value.astype(jnp.float32), dh_blocks)
    start_grad = jnp.zeros((n_slice, SLOTS, BLOCK, BLOCK), jnp.float32)
    w_grad, dh_all = lax.scan(advance, start_grad, (hidden_groups, cot_groups))
    d_hidden = dh_all.reshape(TOKENS, FF).astype(jnp.bfloat16)
    dh_f = d_hidden.astype(jnp.float32)
    d_gate = (dh_f * up_f * (gate_sig * (1.0 + gate_f * (1.0 - gate_sig)))).astype(jnp.bfloat16)
    d_up = (dh_f * (gate_f * gate_sig)).astype(jnp.bfloat16)
    return (d_gate, d_up, w_grad)
```

```python
import functools
import math

import jax
import jax.numpy as jnp
from jax import lax
from jax.experimental import pallas as pl
from jax.experimental.pallas import tpu as pltpu
from jax.sharding import PartitionSpec as P

X_CHIPS = 4
GROUP = 16


def pack_kernel(gate_ref, up_ref, out_ref):
    out_ref[0, 0] = gate_ref[...]
    out_ref[0, 1] = up_ref[...]


def pack(gate, up, parts):
    rows, width = gate.shape
    cols = width // parts
    return pl.pallas_call(
        pack_kernel,
        grid=(parts,),
        in_specs=[pl.BlockSpec((rows, cols), lambda i: (0, i))] * 2,
        out_specs=pl.BlockSpec((1, 2, rows, cols), lambda i: (i, 0, 0, 0)),
        out_shape=jax.ShapeDtypeStruct((parts, 2, rows, cols), gate.dtype),
        cost_estimate=pl.CostEstimate(flops=0, bytes_accessed=8 * rows * width, transcendentals=0),
        name="pack",
    )(gate, up)


def unpack_kernel(in_ref, gate_ref, up_ref):
    gate_ref[...] = in_ref[0, 0]
    up_ref[...] = in_ref[0, 1]


def unpack(packed):
    parts, _, rows, cols = packed.shape
    shape = jax.ShapeDtypeStruct((rows, parts * cols), packed.dtype)
    return pl.pallas_call(
        unpack_kernel,
        grid=(parts,),
        in_specs=[pl.BlockSpec((1, 2, rows, cols), lambda i: (i, 0, 0, 0))],
        out_specs=[pl.BlockSpec((rows, cols), lambda i: (0, i))] * 2,
        out_shape=[shape, shape],
        cost_estimate=pl.CostEstimate(flops=0, bytes_accessed=8 * rows * parts * cols, transcendentals=0),
        name="unpack",
    )(packed)


def partial_kernel(scale, ids_ref, act_ref, dy_ref, out_ref, hidden_t):
    step = pl.program_id(0)
    parts, _, rows, cols = act_ref.shape
    block = out_ref.shape[1]
    col_bits = (dy_ref.shape[1] // block).bit_length() - 1

    @pl.when(step == 0)
    def _():
        for r in range(cols // block):
            span = slice(r * block, (r + 1) * block)
            pieces = []
            for p in range(parts):
                gate = act_ref[p, 0, :, span].astype(jnp.float32)
                up = act_ref[p, 1, :, span].astype(jnp.float32)
                pieces.append(gate * jax.nn.sigmoid(gate) * up)
            hidden_t[r] = jnp.concatenate(pieces, axis=0).T.astype(jnp.bfloat16)

    for k in range(out_ref.shape[0]):
        slot = ids_ref[step * out_ref.shape[0] + k]
        safe = jnp.maximum(slot, 0)
        factor = jnp.where(slot >= 0, jnp.float32(scale), jnp.float32(0))
        row = safe >> col_bits
        col = pl.multiple_of((safe & ((1 << col_bits) - 1)) * block, block)
        product = jnp.dot(
            hidden_t[row], dy_ref[:, pl.ds(col, block)], preferred_element_type=jnp.float32
        )
        out_ref[k] = (product * factor).astype(jnp.bfloat16)


def partial_blocks(ids, act, dy, block, scale):
    parts, _, rows, cols = act.shape
    slots = ids.shape[0]
    tokens = parts * rows
    return pl.pallas_call(
        functools.partial(partial_kernel, scale),
        grid_spec=pltpu.PrefetchScalarGridSpec(
            num_scalar_prefetch=1,
            grid=(slots // GROUP,),
            in_specs=[
                pl.BlockSpec(act.shape, lambda i, ids: (0, 0, 0, 0)),
                pl.BlockSpec(dy.shape, lambda i, ids: (0, 0)),
            ],
            out_specs=pl.BlockSpec((GROUP, block, block), lambda i, ids: (i, 0, 0)),
            scratch_shapes=[pltpu.VMEM((cols // block, block, tokens), jnp.bfloat16)],
        ),
        out_shape=jax.ShapeDtypeStruct((slots, block, block), jnp.bfloat16),
        cost_estimate=pl.CostEstimate(
            flops=2 * slots * tokens * block * block,
            bytes_accessed=2 * (act.size + dy.size + slots * block * block),
            transcendentals=tokens * cols,
        ),
        name="partial_blocks",
    )(ids, act, dy)


def grads_kernel(ids_ref, act_ref, dy_ref, w_ref, out_ref, total):
    step = pl.program_id(0)
    parts, _, rows, cols = act_ref.shape
    block = w_ref.shape[1]
    row_count = cols // block
    col_bits = (dy_ref.shape[1] // block).bit_length() - 1

    @pl.when(step == 0)
    def _():
        total[...] = jnp.zeros_like(total)

    for k in range(w_ref.shape[0]):
        slot = ids_ref[step * w_ref.shape[0] + k]
        safe = jnp.maximum(slot, 0)
        row = jnp.where(slot >= 0, safe >> col_bits, row_count)
        col = pl.multiple_of((safe & ((1 << col_bits) - 1)) * block, block)
        total[row] += lax.dot_general(
            dy_ref[:, pl.ds(col, block)],
            w_ref[k],
            (((1,), (1,)), ((), ())),
            preferred_element_type=jnp.float32,
        )

    @pl.when(step == pl.num_programs(0) - 1)
    def _():
        for r in range(row_count):
            span = slice(r * block, (r + 1) * block)
            for p in range(parts):
                dh = total[r, p * rows : (p + 1) * rows, :]
                dh = dh.astype(jnp.bfloat16).astype(jnp.float32)
                gate = act_ref[p, 0, :, span].astype(jnp.float32)
                up = act_ref[p, 1, :, span].astype(jnp.float32)
                sig = jax.nn.sigmoid(gate)
                out_ref[p, 0, :, span] = (dh * up * (sig * (1.0 + gate * (1.0 - sig)))).astype(
                    jnp.bfloat16
                )
                out_ref[p, 1, :, span] = (dh * (gate * sig)).astype(jnp.bfloat16)


def activation_grads(ids, act, dy, weights):
    parts, _, rows, cols = act.shape
    slots, block, _ = weights.shape
    tokens = parts * rows
    return pl.pallas_call(
        grads_kernel,
        grid_spec=pltpu.PrefetchScalarGridSpec(
            num_scalar_prefetch=1,
            grid=(slots // GROUP,),
            in_specs=[
                pl.BlockSpec(act.shape, lambda i, ids: (0, 0, 0, 0)),
                pl.BlockSpec(dy.shape, lambda i, ids: (0, 0)),
                pl.BlockSpec((GROUP, block, block), lambda i, ids: (i, 0, 0)),
            ],
            out_specs=pl.BlockSpec(act.shape, lambda i, ids: (0, 0, 0, 0)),
            scratch_shapes=[pltpu.VMEM((cols // block + 1, tokens, block), jnp.float32)],
        ),
        out_shape=jax.ShapeDtypeStruct(act.shape, jnp.bfloat16),
        cost_estimate=pl.CostEstimate(
            flops=2 * slots * tokens * block * block,
            bytes_accessed=2 * (2 * act.size + dy.size + weights.size),
            transcendentals=tokens * cols,
        ),
        name="activation_grads",
    )(ids, act, dy, weights)


def body(gate_pre, up_pre, cotangent, w_slots, slot_ids):
    n_fsdp = lax.axis_size("fsdp")
    n_tensor = lax.axis_size("tensor")
    n_x, n_z = X_CHIPS, n_fsdp // X_CHIPS
    cap, block = w_slots.shape[1], w_slots.shape[2]
    x_groups = [[x * n_z + z for x in range(n_x)] for z in range(n_z)]
    z_groups = [[x * n_z + z for z in range(n_z)] for x in range(n_x)]
    ids = slot_ids[0]
    weights = lax.all_gather(w_slots[0], "fsdp", axis=0, tiled=True)
    act = lax.all_to_all(
        pack(gate_pre, up_pre, n_tensor), "tensor", split_axis=0, concat_axis=0, tiled=True
    )
    grad_scale = 1.0 / math.sqrt(cotangent.shape[0] * n_fsdp)
    partials = partial_blocks(ids, act, cotangent, block, grad_scale)
    along_x = lax.all_to_all(
        partials, "fsdp", split_axis=0, concat_axis=0, tiled=True, axis_index_groups=x_groups
    )
    summed = (
        along_x.reshape(n_x, n_z * cap, block, block)
        .astype(jnp.float32)
        .sum(axis=0)
        .astype(jnp.bfloat16)
    )
    along_z = lax.all_to_all(
        summed, "fsdp", split_axis=0, concat_axis=0, tiled=True, axis_index_groups=z_groups
    )
    w_grad = along_z.reshape(n_z, cap, block, block).astype(jnp.float32).sum(axis=0)[None]
    grads = activation_grads(ids, act, cotangent, weights)
    grads = lax.all_to_all(grads, "tensor", split_axis=0, concat_axis=0, tiled=True)
    d_gate, d_up = unpack(grads)
    return (d_gate, d_up, w_grad)


def solution(mesh):
    placed = (
        P(("fsdp", "tensor"), None),
        P(("fsdp", "tensor"), None),
        P("fsdp", None),
        P("tensor", "fsdp", None, None),
        P("tensor", None),
    )
    return jax.shard_map(
        body,
        mesh=mesh,
        in_specs=placed,
        out_specs=(
            P(("fsdp", "tensor"), None),
            P(("fsdp", "tensor"), None),
            P("tensor", "fsdp", None, None),
        ),
        check_vma=False,
    )
```

```python
import functools
import math

import jax
import jax.numpy as jnp
from jax import lax
from jax.experimental import pallas as pl
from jax.experimental.pallas import tpu as pltpu
from jax.sharding import PartitionSpec as P

X_CHIPS = 4
STRIDE = 4


def pack_kernel(gate_ref, up_ref, out_ref):
    out_ref[0, 0] = gate_ref[...]
    out_ref[0, 1] = up_ref[...]


def pack(gate, up, parts):
    rows, width = gate.shape
    cols = width // parts
    return pl.pallas_call(
        pack_kernel,
        grid=(parts,),
        in_specs=[pl.BlockSpec((rows, cols), lambda i: (0, i))] * 2,
        out_specs=pl.BlockSpec((1, 2, rows, cols), lambda i: (i, 0, 0, 0)),
        out_shape=jax.ShapeDtypeStruct((parts, 2, rows, cols), gate.dtype),
        cost_estimate=pl.CostEstimate(flops=0, bytes_accessed=8 * rows * width, transcendentals=0),
        name="pack",
    )(gate, up)


def unpack_kernel(in_ref, gate_ref, up_ref):
    gate_ref[...] = in_ref[0, 0]
    up_ref[...] = in_ref[0, 1]


def unpack(packed):
    parts, _, rows, cols = packed.shape
    shape = jax.ShapeDtypeStruct((rows, parts * cols), packed.dtype)
    return pl.pallas_call(
        unpack_kernel,
        grid=(parts,),
        in_specs=[pl.BlockSpec((1, 2, rows, cols), lambda i: (i, 0, 0, 0))],
        out_specs=[pl.BlockSpec((rows, cols), lambda i: (0, i))] * 2,
        out_shape=[shape, shape],
        cost_estimate=pl.CostEstimate(flops=0, bytes_accessed=8 * rows * parts * cols, transcendentals=0),
        name="unpack",
    )(packed)


def partial_kernel(scale, first, x_base, stride, cap, *refs):
    if first:
        ids_ref, parity_ref, act_ref, dy_ref, out_ref, hidden_t = refs
    else:
        ids_ref, parity_ref, hidden_t, dy_ref, out_ref = refs
    step = pl.program_id(0)
    group, block = out_ref.shape[0], out_ref.shape[1]
    halves = stride // 2
    per_x = ids_ref.shape[0] // X_CHIPS
    col_bits = (dy_ref.shape[1] // block).bit_length() - 1

    if first:

        @pl.when(step == 0)
        def _():
            parts, _, rows, cols = act_ref.shape
            for r in range(cols // block):
                span = slice(r * block, (r + 1) * block)
                pieces = []
                for p in range(parts):
                    gate = act_ref[p, 0, :, span].astype(jnp.float32)
                    up = act_ref[p, 1, :, span].astype(jnp.float32)
                    pieces.append(gate * jax.nn.sigmoid(gate) * up)
                hidden_t[r] = jnp.concatenate(pieces, axis=0).T.astype(jnp.bfloat16)

    base = (x_base + step // halves) * per_x + ((step % halves) * 2 + parity_ref[0]) * cap
    for k in range(group):
        slot = ids_ref[base + (k // cap) * stride * cap + k % cap]
        safe = jnp.maximum(slot, 0)
        factor = jnp.where(slot >= 0, jnp.float32(scale), jnp.float32(0))
        row = safe >> col_bits
        col = pl.multiple_of((safe & ((1 << col_bits) - 1)) * block, block)
        product = jnp.dot(
            hidden_t[row], dy_ref[:, pl.ds(col, block)], preferred_element_type=jnp.float32
        )
        out_ref[k] = (product * factor).astype(jnp.bfloat16)


def partial_blocks(ids, parity, source, dy, block, cap, scale, x_base, x_count, first):
    slots = ids.shape[0]
    group = slots // (X_CHIPS * STRIDE)
    steps = x_count * STRIDE // 2
    tokens = dy.shape[0]
    if first:
        rows = source.shape[3] // block
    else:
        rows = source.shape[0]
    zeros = lambda n: (lambda i, *_: (0,) * n)
    out_specs = [pl.BlockSpec((group, block, block), lambda i, *_: (i, 0, 0))]
    out_shape = [jax.ShapeDtypeStruct((steps * group, block, block), jnp.bfloat16)]
    if first:
        out_specs.append(pl.BlockSpec((rows, block, tokens), zeros(3)))
        out_shape.append(jax.ShapeDtypeStruct((rows, block, tokens), jnp.bfloat16))
    return pl.pallas_call(
        functools.partial(partial_kernel, scale, first, x_base, STRIDE, cap),
        grid_spec=pltpu.PrefetchScalarGridSpec(
            num_scalar_prefetch=2,
            grid=(steps,),
            in_specs=[
                pl.BlockSpec(source.shape, zeros(len(source.shape))),
                pl.BlockSpec(dy.shape, zeros(2)),
            ],
            out_specs=out_specs,
        ),
        out_shape=out_shape,
        cost_estimate=pl.CostEstimate(
            flops=2 * steps * group * tokens * block * block,
            bytes_accessed=2 * (source.size + dy.size + steps * group * block * block),
            transcendentals=tokens * rows * block if first else 0,
        ),
        name="partial_blocks",
    )(ids, parity, source, dy)


def pair_sum_kernel(keep_ref, up_ref, down_ref, out_ref):
    half = pl.num_programs(0) // 2

    @pl.when(pl.program_id(0) < half)
    def _():
        out_ref[...] = (
            keep_ref[...].astype(jnp.float32) + up_ref[...].astype(jnp.float32)
        ).astype(out_ref.dtype)

    @pl.when(pl.program_id(0) >= half)
    def _():
        out_ref[...] = (
            keep_ref[...].astype(jnp.float32) + down_ref[...].astype(jnp.float32)
        ).astype(out_ref.dtype)


def pair_sum(keep, up, down, steps):
    n, block, _ = keep.shape
    size = (n // steps, block, block)
    half = steps // 2
    return pl.pallas_call(
        pair_sum_kernel,
        grid=(steps,),
        in_specs=[
            pl.BlockSpec(size, lambda i: (i, 0, 0)),
            pl.BlockSpec(size, lambda i: (jnp.minimum(i, half - 1), 0, 0)),
            pl.BlockSpec(size, lambda i: (jnp.maximum(i - half, 0), 0, 0)),
        ],
        out_specs=pl.BlockSpec(size, lambda i: (i, 0, 0)),
        out_shape=jax.ShapeDtypeStruct(keep.shape, jnp.bfloat16),
        cost_estimate=pl.CostEstimate(flops=keep.size, bytes_accessed=6 * keep.size, transcendentals=0),
        name="pair_sum",
    )(keep, up, down)


def x_sum_kernel(bit_ref, in_ref, up_ref, down_ref, keep_ref):
    n = keep_ref.shape[0]
    bit = bit_ref[0]
    far = (1 - bit) * n
    near = bit * n

    def total(at):
        value = in_ref[0, at].astype(jnp.float32)
        for x in range(1, in_ref.shape[0]):
            value = value + in_ref[x, at].astype(jnp.float32)
        return value

    for k in range(n // 2):
        up_ref[k] = total(far + k).astype(jnp.bfloat16)
        down_ref[k] = total(far + n // 2 + k).astype(jnp.bfloat16)
    for k in range(n):
        keep_ref[k] = total(near + k)


def x_sum(bit, stacked):
    _, n, block, _ = stacked.shape
    half = jax.ShapeDtypeStruct((n // 4, block, block), jnp.bfloat16)
    return pl.pallas_call(
        x_sum_kernel,
        in_specs=[
            pl.BlockSpec(memory_space=pltpu.SMEM),
            pl.BlockSpec(memory_space=pltpu.VMEM),
        ],
        out_specs=[pl.BlockSpec(memory_space=pltpu.VMEM)] * 3,
        out_shape=[half, half, jax.ShapeDtypeStruct((n // 2, block, block), jnp.float32)],
        cost_estimate=pl.CostEstimate(
            flops=stacked.size, bytes_accessed=3 * stacked.size, transcendentals=0
        ),
        name="x_sum",
    )(bit, stacked)


def grads_kernel(x_steps, bases, n_z, last, ids_ref, place_ref, *refs):
    count = len(x_steps)
    pieces = refs[:count]
    if last:
        dy_ref, act_ref, given, out_ref, total = refs[count:]
    else:
        dy_ref, total = refs[count:]
    block = pieces[0].shape[1]
    row_count = total.shape[0] - 1
    cap = pieces[0].shape[0] * 2 // n_z
    col_bits = (dy_ref.shape[1] // block).bit_length() - 1
    if last:
        total[...] = given[...]
    else:
        total[...] = jnp.zeros_like(total)

    for piece, x_step, base in zip(pieces, x_steps, bases):
        x_at = ((place_ref[0] + x_step) & (X_CHIPS - 1)) * n_z

        def advance(i, carry, piece=piece, x_at=x_at, base=base):
            places = []
            products = []
            for u in range(2):
                owner = x_at + ((place_ref[1] + base + 2 * (2 * i + u)) & (n_z - 1))
                for j in range(cap):
                    slot = ids_ref[owner * cap + j]
                    safe = jnp.maximum(slot, 0)
                    places.append(jnp.where(slot >= 0, safe >> col_bits, row_count))
                    col = pl.multiple_of((safe & ((1 << col_bits) - 1)) * block, block)
                    products.append(
                        lax.dot_general(
                            dy_ref[:, pl.ds(col, block)],
                            piece[(2 * i + u) * cap + j],
                            (((1,), (1,)), ((), ())),
                            preferred_element_type=jnp.float32,
                        )
                    )
            for row, product in zip(places, products):
                total[row] += product
            return carry

        lax.fori_loop(0, n_z // 4, advance, 0)

    if last:
        parts, _, rows, _ = act_ref.shape
        for r in range(row_count):
            span = slice(r * block, (r + 1) * block)
            for p in range(parts):
                dh = total[r, p * rows : (p + 1) * rows, :]
                dh = dh.astype(jnp.bfloat16).astype(jnp.float32)
                gate = act_ref[p, 0, :, span].astype(jnp.float32)
                up = act_ref[p, 1, :, span].astype(jnp.float32)
                sig = jax.nn.sigmoid(gate)
                out_ref[p, 0, :, span] = (dh * up * (sig * (1.0 + gate * (1.0 - sig)))).astype(
                    jnp.bfloat16
                )
                out_ref[p, 1, :, span] = (dh * (gate * sig)).astype(jnp.bfloat16)


def block_products(ids, place, pieces, x_steps, bases, dy, rows, n_z, act=None, given=None):
    last = act is not None
    n, block, _ = pieces[0].shape
    tokens = dy.shape[0]
    total = jax.ShapeDtypeStruct((rows + 1, tokens, block), jnp.float32)
    vmem = pl.BlockSpec(memory_space=pltpu.VMEM)
    smem = pl.BlockSpec(memory_space=pltpu.SMEM)
    args = [ids, place, *pieces, dy] + ([act, given] if last else [])
    moved = len(pieces) * n * block * block + dy.size
    return pl.pallas_call(
        functools.partial(grads_kernel, x_steps, bases, n_z, last),
        in_specs=[smem, smem] + [vmem] * (len(args) - 2),
        out_specs=vmem,
        out_shape=jax.ShapeDtypeStruct(act.shape, jnp.bfloat16) if last else total,
        scratch_shapes=[pltpu.VMEM(total.shape, total.dtype)] if last else [],
        cost_estimate=pl.CostEstimate(
            flops=2 * len(pieces) * n * tokens * block * block,
            bytes_accessed=2 * moved + 4 * total.size + (4 * act.size if last else 0),
            transcendentals=act.size // 2 if last else 0,
        ),
        name="block_products",
    )(*args)


def body(gate_pre, up_pre, cotangent, w_slots, slot_ids):
    n_fsdp = lax.axis_size("fsdp")
    n_tensor = lax.axis_size("tensor")
    n_x, n_z = X_CHIPS, n_fsdp // X_CHIPS
    cap, block = w_slots.shape[1], w_slots.shape[2]
    rows = gate_pre.shape[1] // n_tensor // block
    x_groups = [[x * n_z + z for x in range(n_x)] for z in range(n_z)]
    far_groups = [
        [x * n_z + z for z in range(m, n_z, STRIDE)] for x in range(n_x) for m in range(STRIDE)
    ]

    def shift(value, x_by, z_by):
        pairs = [
            (x * n_z + z, (x + x_by) % n_x * n_z + (z + z_by) % n_z)
            for x in range(n_x)
            for z in range(n_z)
        ]
        return lax.ppermute(value, "fsdp", pairs)

    me = lax.axis_index("fsdp")
    place = jnp.stack([me // n_z, me % n_z]).astype(jnp.int32)
    parity = (me % 2).astype(jnp.int32)[None]
    second = (me // 2 % 2).astype(jnp.int32)[None]
    ids = slot_ids[0]

    own = w_slots[0]
    from_4, from_12, from_8 = shift(own, 0, -4), shift(own, 0, 4), shift(own, 0, 8)
    act = lax.all_to_all(
        pack(gate_pre, up_pre, n_tensor), "tensor", split_axis=0, concat_axis=0, tiled=True
    )
    act, from_4, from_12, from_8 = lax.optimization_barrier((act, from_4, from_12, from_8))
    from_2_6 = shift(jnp.concatenate([own, from_4]), 0, -2)
    from_10_14 = shift(jnp.concatenate([from_12, own]), 0, 2)
    scale = 1.0 / math.sqrt(cotangent.shape[0] * n_fsdp)
    send_up, hidden_t = partial_blocks(
        ids, 1 - parity, act, cotangent, block, cap, scale, 0, n_x // 2, True
    )
    hidden_t, from_2_6, from_10_14 = lax.optimization_barrier((hidden_t, from_2_6, from_10_14))
    even = jnp.concatenate(
        [from_10_14[:cap], from_12, from_10_14[cap:], own, from_2_6[:cap], from_4, from_2_6[cap:], from_8]
    )
    even_up, even_down = shift(even, 1, 0), shift(even, -1, 0)
    quarter = n_z // 4 * cap
    odd_down = shift(even[:quarter], 0, 1)
    odd_up = shift(even[quarter - cap : 2 * quarter - cap], 0, -1)
    (send_down,) = partial_blocks(
        ids, 1 - parity, hidden_t, cotangent, block, cap, scale, n_x // 2, n_x // 2, False
    )
    got_up, got_down = shift(send_up, 0, 1), shift(send_down, 0, -1)
    hidden_t, odd_down, odd_up, even_up, even_down = lax.optimization_barrier(
        (hidden_t, odd_down, odd_up, even_up, even_down)
    )
    odd = jnp.concatenate([odd_down, odd_up])
    odd_up, odd_down = shift(odd, 1, 0), shift(odd, -1, 0)
    (keep,) = partial_blocks(ids, parity, hidden_t, cotangent, block, cap, scale, 0, n_x, False)
    keep, odd_up, odd_down, got_up, got_down = lax.optimization_barrier(
        (keep, odd_up, odd_down, got_up, got_down)
    )
    paired = pair_sum(keep, got_up, got_down, 8)
    even_far = shift(even_down, -1, 0)
    odd_far = shift(odd_up, 1, 0)
    along_x = lax.all_to_all(
        paired, "fsdp", split_axis=0, concat_axis=0, tiled=True, axis_index_groups=x_groups
    )
    send_up, send_down, keep = x_sum(second, along_x.reshape(n_x, -1, block, block))
    got = jnp.concatenate([shift(send_up, 0, 2), shift(send_down, 0, -2)])
    fours = (keep + got.astype(jnp.float32)).astype(jnp.bfloat16)
    along_z = lax.all_to_all(
        fours, "fsdp", split_axis=0, concat_axis=0, tiled=True, axis_index_groups=far_groups
    )
    w_grad = along_z.reshape(-1, cap, block, block).astype(jnp.float32).sum(axis=0)[None]

    total = block_products(
        ids,
        place,
        [even, odd, even_down, odd_down, even_up, odd_up],
        (0, 0, 1, 1, 3, 3),
        (10, 9) * 3,
        cotangent,
        rows,
        n_z,
    )
    grads = block_products(
        ids, place, [even_far, odd_far], (2, 2), (10, 9), cotangent, rows, n_z, act, total
    )
    grads = lax.all_to_all(grads, "tensor", split_axis=0, concat_axis=0, tiled=True)
    d_gate, d_up = unpack(grads)
    return (d_gate, d_up, w_grad)


def solution(mesh):
    placed = (
        P(("fsdp", "tensor"), None),
        P(("fsdp", "tensor"), None),
        P("fsdp", None),
        P("tensor", "fsdp", None, None),
        P("tensor", None),
    )
    return jax.shard_map(
        body,
        mesh=mesh,
        in_specs=placed,
        out_specs=(
            P(("fsdp", "tensor"), None),
            P(("fsdp", "tensor"), None),
            P("tensor", "fsdp", None, None),
        ),
        check_vma=False,
    )
```

```python
import functools
import math

import jax
import jax.numpy as jnp
from jax import lax
from jax.experimental import pallas as pl
from jax.experimental.pallas import tpu as pltpu
from jax.sharding import PartitionSpec as P

X_CHIPS = 4
STRIDE = 4
VMEM = pl.BlockSpec(memory_space=pltpu.VMEM)
SMEM = pl.BlockSpec(memory_space=pltpu.SMEM)
ANY = pl.BlockSpec(memory_space=pl.ANY)


def shaped(dtype, *shape):
    return jax.ShapeDtypeStruct(shape, dtype)


def cost(flops, moved, transcendentals=0):
    return pl.CostEstimate(flops=flops, bytes_accessed=moved, transcendentals=transcendentals)


def pack_kernel(gate_ref, up_ref, out_ref):
    cols = out_ref.shape[3]
    for p in range(out_ref.shape[0]):
        out_ref[p, 0] = gate_ref[:, p * cols : (p + 1) * cols]
        out_ref[p, 1] = up_ref[:, p * cols : (p + 1) * cols]


def pack(gate, up, parts):
    rows, width = gate.shape
    cols = width // parts
    steps = 2
    return pl.pallas_call(
        pack_kernel,
        grid=(steps,),
        in_specs=[pl.BlockSpec((rows, width // steps), lambda i: (0, i))] * 2,
        out_specs=pl.BlockSpec((parts // steps, 2, rows, cols), lambda i: (i, 0, 0, 0)),
        out_shape=shaped(gate.dtype, parts, 2, rows, cols),
        cost_estimate=cost(0, 8 * rows * width),
        name="pack",
    )(gate, up)


def unpack_kernel(in_ref, gate_ref, up_ref):
    cols = in_ref.shape[3]
    for p in range(in_ref.shape[0]):
        gate_ref[:, p * cols : (p + 1) * cols] = in_ref[p, 0]
        up_ref[:, p * cols : (p + 1) * cols] = in_ref[p, 1]


def unpack(packed):
    parts, _, rows, cols = packed.shape
    steps = 2
    shape = shaped(packed.dtype, rows, parts * cols)
    return pl.pallas_call(
        unpack_kernel,
        grid=(steps,),
        in_specs=[pl.BlockSpec((parts // steps, 2, rows, cols), lambda i: (i, 0, 0, 0))],
        out_specs=[pl.BlockSpec((rows, parts * cols // steps), lambda i: (0, i))] * 2,
        out_shape=[shape, shape],
        cost_estimate=cost(0, 8 * rows * parts * cols),
        name="unpack",
    )(packed)


def hidden_kernel(act_ref, out_ref):
    rows = act_ref.shape[2]
    for p in range(act_ref.shape[0]):
        gate = act_ref[p, 0].astype(jnp.float32)
        up = act_ref[p, 1].astype(jnp.float32)
        out_ref[p * rows : (p + 1) * rows, :] = (gate * jax.nn.sigmoid(gate) * up).astype(
            jnp.bfloat16
        )


def hidden_of(act):
    parts, _, rows, cols = act.shape
    return pl.pallas_call(
        hidden_kernel,
        in_specs=[VMEM],
        out_specs=VMEM,
        out_shape=shaped(jnp.bfloat16, parts * rows, cols),
        cost_estimate=cost(4 * act.size, 3 * act.size, act.size // 2),
        name="hidden",
    )(act)


def fetch(pieces, whole, sem):
    at = 0
    copies = []
    for k, piece in enumerate(pieces):
        rows = piece.shape[0]
        copies.append(pltpu.make_async_copy(piece, whole.at[pl.ds(at, rows)], sem.at[k]))
        at += rows
    for copy in copies:
        copy.start()
    return copies


def place_of(slot, col_bits, block):
    safe = jnp.maximum(slot, 0)
    col = pl.multiple_of((safe & ((1 << col_bits) - 1)) * block, block)
    return safe >> col_bits, col


def products_kernel(n_z, cap, n_pieces, ids_ref, at_ref, *refs):
    dy_pieces = refs[:n_pieces]
    even_ref, odd_ref = refs[n_pieces : n_pieces + 2]
    own_ref, right_ref, left_ref, top_ref, bottom_ref, dy, total, sem = refs[n_pieces + 2 :]
    row_count, tokens, block = own_ref.shape
    col_bits = (dy.shape[1] // block).bit_length() - 1
    copies = fetch(dy_pieces, dy, sem)
    total[...] = jnp.zeros_like(total)
    for copy in copies:
        copy.wait()
    start = at_ref[0] * n_z
    for piece, base in ((even_ref, n_z // 2 + 2), (odd_ref, n_z // 2 + 1)):

        def advance(i, carry, piece=piece, base=base):
            owner = start + ((at_ref[1] + base + 2 * i) & (n_z - 1))
            rows, products = [], []
            for j in range(cap):
                slot = ids_ref[owner * cap + j]
                row, col = place_of(slot, col_bits, block)
                rows.append(jnp.where(slot >= 0, row, row_count))
                products.append(
                    lax.dot_general(
                        dy[:, pl.ds(col, block)],
                        piece[i * cap + j],
                        (((1,), (1,)), ((), ())),
                        preferred_element_type=jnp.float32,
                    )
                )
            for row, product in zip(rows, products):
                total[row] += product
            return carry

        lax.fori_loop(0, n_z // 2, advance, 0)
    half = tokens // 2
    for r in range(row_count):
        own_ref[r] = total[r, :tokens]
        right_ref[r] = total[r, tokens : 2 * tokens].astype(jnp.bfloat16)
        left_ref[r] = total[r, 2 * tokens : 3 * tokens].astype(jnp.bfloat16)
        top_ref[r] = total[r, 3 * tokens : 3 * tokens + half].astype(jnp.bfloat16)
        bottom_ref[r] = total[r, 3 * tokens + half :].astype(jnp.bfloat16)


def block_products(ids, at, dy_pieces, even, odd, rows, n_z, cap):
    tokens, width = dy_pieces[0].shape
    block = even.shape[1]
    whole = tokens * X_CHIPS
    half = shaped(jnp.bfloat16, rows, tokens // 2, block)
    full = shaped(jnp.bfloat16, rows, tokens, block)
    return pl.pallas_call(
        functools.partial(products_kernel, n_z, cap, len(dy_pieces)),
        in_specs=[SMEM, SMEM] + [ANY] * len(dy_pieces) + [VMEM] * 2,
        out_specs=[VMEM] * 5,
        out_shape=[shaped(jnp.float32, rows, tokens, block), full, full, half, half],
        scratch_shapes=[
            pltpu.VMEM((whole, width), jnp.bfloat16),
            pltpu.VMEM((rows + 1, whole, block), jnp.float32),
            pltpu.SemaphoreType.DMA((len(dy_pieces),)),
        ],
        cost_estimate=cost(
            4 * even.size * whole, 2 * whole * width + 4 * even.size + 10 * rows * tokens * block
        ),
        name="block_products",
    )(ids, at, *dy_pieces, even, odd)


def partials_kernel(scale, n_z, cap, n_pieces, ids_ref, at_ref, *refs):
    dy_pieces = refs[:n_pieces]
    hidden_pieces = refs[n_pieces : 2 * n_pieces]
    up_ref, down_ref, keep_ref, dy, hidden_t, sem = refs[2 * n_pieces :]
    row_count, block, _ = hidden_t.shape
    col_bits = (dy.shape[1] // block).bit_length() - 1
    copies = fetch(dy_pieces, dy, sem)
    at = 0
    for piece in hidden_pieces:
        tokens = piece.shape[0]
        for r in range(row_count):
            value = piece[:, r * block : (r + 1) * block].astype(jnp.float32)
            hidden_t[r, :, at : at + tokens] = value.T.astype(jnp.bfloat16)
        at += tokens
    for copy in copies:
        copy.wait()
    quarter = n_z // STRIDE
    for sending in (1, 0):
        parity = (at_ref[1] + sending) & 1

        def advance(i, carry, sending=sending, parity=parity):
            for q in range(2):
                for j in range(cap):
                    owner = at_ref[0] * n_z + i * STRIDE + 2 * q + parity
                    slot = ids_ref[owner * cap + j]
                    row, col = place_of(slot, col_bits, block)
                    factor = jnp.where(slot >= 0, jnp.float32(scale), jnp.float32(0))
                    value = factor * jnp.dot(
                        hidden_t[row], dy[:, pl.ds(col, block)], preferred_element_type=jnp.float32
                    )
                    if sending:
                        (down_ref if q else up_ref)[i * cap + j] = value.astype(jnp.bfloat16)
                    else:
                        keep_ref[q * quarter * cap + i * cap + j] = value
            return carry

        lax.fori_loop(0, quarter, advance, 0)


def partial_blocks(ids, at, dy_pieces, hidden_pieces, block, n_z, cap, scale):
    tokens, width = dy_pieces[0].shape
    whole = tokens * X_CHIPS
    rows = hidden_pieces[0].shape[1] // block
    part = n_z // 4 * cap
    return pl.pallas_call(
        functools.partial(partials_kernel, scale, n_z, cap, len(dy_pieces)),
        in_specs=[SMEM, SMEM] + [ANY] * len(dy_pieces) + [VMEM] * len(hidden_pieces),
        out_specs=[VMEM] * 3,
        out_shape=[
            shaped(jnp.bfloat16, part, block, block),
            shaped(jnp.bfloat16, part, block, block),
            shaped(jnp.float32, 2 * part, block, block),
        ],
        scratch_shapes=[
            pltpu.VMEM((whole, width), jnp.bfloat16),
            pltpu.VMEM((rows, block, whole), jnp.bfloat16),
            pltpu.SemaphoreType.DMA((len(dy_pieces),)),
        ],
        cost_estimate=cost(
            8 * part * block * block * whole, 2 * whole * (width + rows * block)
        ),
        name="partial_blocks",
    )(ids, at, *dy_pieces, *hidden_pieces)


def second_kernel(at_ref, keep_ref, up_ref, down_ref, up_out, down_out, keep_out):
    part = up_ref.shape[0]
    half = part // 2
    bit = (at_ref[1] >> 1) & 1
    first = lambda k: keep_ref[k] + up_ref[k].astype(jnp.float32)
    other = lambda k: keep_ref[part + k] + down_ref[k].astype(jnp.float32)
    for value, (near, far) in enumerate(((first, other), (other, first))):

        @pl.when(bit == value)
        def _(near=near, far=far):
            for k in range(half):
                up_out[k] = far(k).astype(jnp.bfloat16)
                down_out[k] = far(half + k).astype(jnp.bfloat16)
            for k in range(part):
                keep_out[k] = near(k)


def second_stage(at, keep, up, down):
    part, block, _ = up.shape
    half = shaped(jnp.bfloat16, part // 2, block, block)
    return pl.pallas_call(
        second_kernel,
        in_specs=[SMEM] + [VMEM] * 3,
        out_specs=[VMEM] * 3,
        out_shape=[half, half, shaped(jnp.float32, part, block, block)],
        cost_estimate=cost(2 * up.size, 18 * up.size),
        name="second_stage",
    )(at, keep, up, down)


def third_kernel(cap, at_ref, keep_ref, up_ref, down_ref, own_out, *rest):
    outs, total = rest[:-1], rest[-1]
    half = up_ref.shape[0]
    for k in range(half):
        total[k] = keep_ref[k] + up_ref[k].astype(jnp.float32)
        total[half + k] = keep_ref[half + k] + down_ref[k].astype(jnp.float32)
    count = 2 * half // cap
    mine = at_ref[1] // STRIDE
    for j in range(cap):
        own_out[j] = total[mine * cap + j]
        for d, out in enumerate(outs):
            out[j] = total[((mine + 1 + d) & (count - 1)) * cap + j].astype(jnp.bfloat16)


def third_stage(at, keep, up, down, cap):
    part, block, _ = keep.shape
    piece = shaped(jnp.bfloat16, cap, block, block)
    return pl.pallas_call(
        functools.partial(third_kernel, cap),
        in_specs=[SMEM] + [VMEM] * 3,
        out_specs=[VMEM] * (part // cap),
        out_shape=[shaped(jnp.float32, cap, block, block)] + [piece] * (part // cap - 1),
        scratch_shapes=[pltpu.VMEM(keep.shape, jnp.float32)],
        cost_estimate=cost(keep.size, 10 * keep.size),
        name="third_stage",
    )(at, keep, up, down)


def grads_kernel(own_ref, left_ref, right_ref, top_ref, bottom_ref, act_ref, out_ref):
    row_count, tokens, block = own_ref.shape
    parts, _, rows, _ = act_ref.shape
    half = tokens // 2
    for r in range(row_count):
        span = slice(r * block, (r + 1) * block)
        for p in range(parts):
            here = slice(p * rows, (p + 1) * rows)
            low = p * rows < half
            across = top_ref if low else bottom_ref
            there = here if low else slice(p * rows - half, (p + 1) * rows - half)
            dh = (
                own_ref[r, here]
                + left_ref[r, here].astype(jnp.float32)
                + right_ref[r, here].astype(jnp.float32)
                + across[r, there].astype(jnp.float32)
            )
            dh = dh.astype(jnp.bfloat16).astype(jnp.float32)
            gate = act_ref[p, 0, :, span].astype(jnp.float32)
            up = act_ref[p, 1, :, span].astype(jnp.float32)
            sig = jax.nn.sigmoid(gate)
            out_ref[p, 0, :, span] = (dh * up * (sig * (1.0 + gate * (1.0 - sig)))).astype(
                jnp.bfloat16
            )
            out_ref[p, 1, :, span] = (dh * (gate * sig)).astype(jnp.bfloat16)


def activation_grads(own, left, right, top, bottom, act):
    return pl.pallas_call(
        grads_kernel,
        in_specs=[VMEM] * 6,
        out_specs=VMEM,
        out_shape=shaped(jnp.bfloat16, *act.shape),
        cost_estimate=cost(8 * act.size, 10 * own.size + 4 * act.size, act.size // 2),
        name="activation_grads",
    )(own, left, right, top, bottom, act)


def body(gate_pre, up_pre, cotangent, w_slots, slot_ids):
    n_fsdp = lax.axis_size("fsdp")
    n_tensor = lax.axis_size("tensor")
    n_x, n_z = X_CHIPS, n_fsdp // X_CHIPS
    cap, block = w_slots.shape[1], w_slots.shape[2]
    rows = gate_pre.shape[1] // n_tensor // block
    half = cotangent.shape[0] // 2
    together = lax.optimization_barrier

    def shift(value, x_by, z_by):
        pairs = [
            (x * n_z + z, (x + x_by) % n_x * n_z + (z + z_by) % n_z)
            for x in range(n_x)
            for z in range(n_z)
        ]
        return lax.ppermute(value, "fsdp", pairs)

    me = lax.axis_index("fsdp")
    at = jnp.stack([me // n_z, me % n_z]).astype(jnp.int32)
    ids = slot_ids[0]
    own = w_slots[0]

    dy_right, dy_left = shift(cotangent, -1, 0), shift(cotangent, 1, 0)
    from_4, from_12, from_8 = shift(own, 0, -4), shift(own, 0, 4), shift(own, 0, 8)
    act = lax.all_to_all(
        pack(gate_pre, up_pre, n_tensor), "tensor", split_axis=0, concat_axis=0, tiled=True
    )
    act, from_4, from_12, from_8 = together((act, from_4, from_12, from_8))
    hidden = hidden_of(act)
    hidden, from_4, from_12, from_8 = together((hidden, from_4, from_12, from_8))
    h_right, h_left = shift(hidden, -1, 0), shift(hidden, 1, 0)
    from_2_6 = shift(jnp.concatenate([own, from_4]), 0, -2)
    from_10_14 = shift(jnp.concatenate([from_12, own]), 0, 2)
    dy_top, dy_bottom = shift(dy_right[:half], -1, 0), shift(dy_left[half:], 1, 0)
    even = jnp.concatenate(
        [from_10_14[:cap], from_12, from_10_14[cap:], own, from_2_6[:cap], from_4, from_2_6[cap:], from_8]
    )
    quarter = n_z // 4 * cap
    odd_down = shift(even[:quarter], 0, 1)
    odd_up = shift(even[quarter - cap : 2 * quarter - cap], 0, -1)
    odd = jnp.concatenate([odd_down, odd_up])
    dy_top, dy_bottom, h_right, h_left = together((dy_top, dy_bottom, h_right, h_left))
    h_top, h_bottom = shift(h_right[:half], -1, 0), shift(h_left[half:], 1, 0)

    dys = [cotangent, dy_right, dy_left, dy_top, dy_bottom]
    mine, to_right, to_left, top, bottom = block_products(
        ids, at, dys, even, odd, rows, n_z, cap
    )
    got_left, got_right = shift(to_right, 1, 0), shift(to_left, -1, 0)
    got_top, got_bottom = shift(top, 2, 0), shift(bottom, -2, 0)

    scale = 1.0 / math.sqrt(cotangent.shape[0] * n_fsdp)
    hiddens = [hidden, h_right, h_left, h_top, h_bottom]
    up, down, keep = partial_blocks(ids, at, dys, hiddens, block, n_z, cap, scale)
    got_left, got_right, got_top, got_bottom, up, down, keep = together(
        (got_left, got_right, got_top, got_bottom, up, down, keep)
    )
    up, down, keep = second_stage(at, keep, shift(up, 0, 1), shift(down, 0, -1))
    w_mine, *others = third_stage(at, keep, shift(up, 0, 2), shift(down, 0, -2), cap)
    w_grad = w_mine
    for d, value in enumerate(others):
        w_grad = w_grad + shift(value, 0, STRIDE * (d + 1)).astype(jnp.float32)
    w_grad = w_grad[None]

    grads = activation_grads(mine, got_left, got_right, got_top, got_bottom, act)
    grads = lax.all_to_all(grads, "tensor", split_axis=0, concat_axis=0, tiled=True)
    d_gate, d_up = unpack(grads)
    return (d_gate, d_up, w_grad)


def solution(mesh):
    placed = (
        P(("fsdp", "tensor"), None),
        P(("fsdp", "tensor"), None),
        P("fsdp", None),
        P("tensor", "fsdp", None, None),
        P("tensor", None),
    )
    return jax.shard_map(
        body,
        mesh=mesh,
        in_specs=placed,
        out_specs=(
            P(("fsdp", "tensor"), None),
            P(("fsdp", "tensor"), None),
            P("tensor", "fsdp", None, None),
        ),
        check_vma=False,
    )
```

```python
import functools
import math

import jax
import jax.numpy as jnp
from jax import lax
from jax.experimental import pallas as pl
from jax.experimental.pallas import tpu as pltpu
from jax.sharding import PartitionSpec as P

X_CHIPS = 4
VMEM = pl.BlockSpec(memory_space=pltpu.VMEM)
SMEM = pl.BlockSpec(memory_space=pltpu.SMEM)
ANY = pl.BlockSpec(memory_space=pl.ANY)


def shaped(dtype, *shape):
    return jax.ShapeDtypeStruct(shape, dtype)


def cost(flops, moved, transcendentals=0):
    return pl.CostEstimate(flops=flops, bytes_accessed=moved, transcendentals=transcendentals)


def pack_kernel(gate_ref, up_ref, out_ref):
    cols = out_ref.shape[3]
    for p in range(out_ref.shape[0]):
        out_ref[p, 0] = gate_ref[:, p * cols : (p + 1) * cols]
        out_ref[p, 1] = up_ref[:, p * cols : (p + 1) * cols]


def pack(gate, up, parts):
    rows, width = gate.shape
    cols = width // parts
    steps = 2
    return pl.pallas_call(
        pack_kernel,
        grid=(steps,),
        in_specs=[pl.BlockSpec((rows, width // steps), lambda i: (0, i))] * 2,
        out_specs=pl.BlockSpec((parts // steps, 2, rows, cols), lambda i: (i, 0, 0, 0)),
        out_shape=shaped(gate.dtype, parts, 2, rows, cols),
        cost_estimate=cost(0, 8 * rows * width),
        name="pack",
    )(gate, up)


def unpack_kernel(in_ref, gate_ref, up_ref):
    cols = in_ref.shape[3]
    for p in range(in_ref.shape[0]):
        gate_ref[:, p * cols : (p + 1) * cols] = in_ref[p, 0]
        up_ref[:, p * cols : (p + 1) * cols] = in_ref[p, 1]


def unpack(packed):
    parts, _, rows, cols = packed.shape
    steps = 2
    shape = shaped(packed.dtype, rows, parts * cols)
    return pl.pallas_call(
        unpack_kernel,
        grid=(steps,),
        in_specs=[pl.BlockSpec((parts // steps, 2, rows, cols), lambda i: (i, 0, 0, 0))],
        out_specs=[pl.BlockSpec((rows, parts * cols // steps), lambda i: (0, i))] * 2,
        out_shape=[shape, shape],
        cost_estimate=cost(0, 8 * rows * parts * cols),
        name="unpack",
    )(packed)


def hidden_kernel(act_ref, out_ref):
    rows = act_ref.shape[2]
    for p in range(act_ref.shape[0]):
        gate = act_ref[p, 0].astype(jnp.float32)
        up = act_ref[p, 1].astype(jnp.float32)
        out_ref[p * rows : (p + 1) * rows, :] = (gate * jax.nn.sigmoid(gate) * up).astype(
            jnp.bfloat16
        )


def hidden_of(act):
    parts, _, rows, cols = act.shape
    return pl.pallas_call(
        hidden_kernel,
        in_specs=[VMEM],
        out_specs=VMEM,
        out_shape=shaped(jnp.bfloat16, parts * rows, cols),
        cost_estimate=cost(4 * act.size, 3 * act.size, act.size // 2),
        name="hidden",
    )(act)


def fetch(pieces, whole, sem):
    at = 0
    copies = []
    for k, piece in enumerate(pieces):
        rows = piece.shape[0]
        copies.append(pltpu.make_async_copy(piece, whole.at[pl.ds(at, rows)], sem.at[k]))
        at += rows
    for copy in copies:
        copy.start()
    return copies


def place_of(slot, col_bits, block):
    safe = jnp.maximum(slot, 0)
    col = pl.multiple_of((safe & ((1 << col_bits) - 1)) * block, block)
    return safe >> col_bits, col


def products_kernel(n_z, cap, n_pieces, ids_ref, at_ref, *refs):
    dy_pieces = refs[:n_pieces]
    w_ref, own_ref, right_ref, left_ref, top_ref, bottom_ref, dy, total, sem = refs[n_pieces:]
    row_count, tokens, block = own_ref.shape
    col_bits = (dy.shape[1] // block).bit_length() - 1
    copies = fetch(dy_pieces, dy, sem)
    total[...] = jnp.zeros_like(total)
    for copy in copies:
        copy.wait()
    start = at_ref[0] * n_z * cap

    def advance(i, carry):
        rows, products = [], []
        for j in range(cap):
            slot = ids_ref[start + i * cap + j]
            row, col = place_of(slot, col_bits, block)
            rows.append(jnp.where(slot >= 0, row, row_count))
            products.append(
                lax.dot_general(
                    dy[:, pl.ds(col, block)],
                    w_ref[i * cap + j],
                    (((1,), (1,)), ((), ())),
                    preferred_element_type=jnp.float32,
                )
            )
        for row, product in zip(rows, products):
            total[row] += product
        return carry

    lax.fori_loop(0, n_z, advance, 0)
    half = tokens // 2
    for r in range(row_count):
        own_ref[r] = total[r, :tokens]
        right_ref[r] = total[r, tokens : 2 * tokens].astype(jnp.bfloat16)
        left_ref[r] = total[r, 2 * tokens : 3 * tokens].astype(jnp.bfloat16)
        top_ref[r] = total[r, 3 * tokens : 3 * tokens + half].astype(jnp.bfloat16)
        bottom_ref[r] = total[r, 3 * tokens + half :].astype(jnp.bfloat16)


def block_products(ids, at, dy_pieces, weights, rows, n_z, cap):
    tokens, width = dy_pieces[0].shape
    block = weights.shape[1]
    whole = tokens * X_CHIPS
    half = shaped(jnp.bfloat16, rows, tokens // 2, block)
    full = shaped(jnp.bfloat16, rows, tokens, block)
    return pl.pallas_call(
        functools.partial(products_kernel, n_z, cap, len(dy_pieces)),
        in_specs=[SMEM, SMEM] + [ANY] * len(dy_pieces) + [VMEM],
        out_specs=[VMEM] * 5,
        out_shape=[shaped(jnp.float32, rows, tokens, block), full, full, half, half],
        scratch_shapes=[
            pltpu.VMEM((whole, width), jnp.bfloat16),
            pltpu.VMEM((rows + 1, whole, block), jnp.float32),
            pltpu.SemaphoreType.DMA((len(dy_pieces),)),
        ],
        cost_estimate=cost(
            2 * weights.size * whole, 2 * whole * width + 2 * weights.size + 10 * rows * tokens * block
        ),
        name="block_products",
    )(ids, at, *dy_pieces, weights)


def partials_kernel(scale, n_z, cap, n_pieces, ids_ref, at_ref, *refs):
    dy_pieces = refs[:n_pieces]
    hidden_pieces = refs[n_pieces : 2 * n_pieces]
    out_ref, dy, hidden_t, sem = refs[2 * n_pieces :]
    row_count, block, _ = hidden_t.shape
    col_bits = (dy.shape[1] // block).bit_length() - 1
    copies = fetch(dy_pieces, dy, sem)
    at = 0
    for piece in hidden_pieces:
        tokens = piece.shape[0]
        for r in range(row_count):
            value = piece[:, r * block : (r + 1) * block].astype(jnp.float32)
            hidden_t[r, :, at : at + tokens] = value.T.astype(jnp.bfloat16)
        at += tokens
    for copy in copies:
        copy.wait()
    start = at_ref[0] * n_z * cap
    group = 2 * cap

    def advance(i, carry):
        for j in range(group):
            slot = ids_ref[start + i * group + j]
            row, col = place_of(slot, col_bits, block)
            factor = jnp.where(slot >= 0, jnp.float32(scale), jnp.float32(0))
            value = factor * jnp.dot(
                hidden_t[row], dy[:, pl.ds(col, block)], preferred_element_type=jnp.float32
            )
            out_ref[i * group + j] = value.astype(jnp.bfloat16)
        return carry

    lax.fori_loop(0, n_z // 2, advance, 0)


def partial_blocks(ids, at, dy_pieces, hidden_pieces, block, n_z, cap, scale):
    tokens, width = dy_pieces[0].shape
    whole = tokens * X_CHIPS
    rows = hidden_pieces[0].shape[1] // block
    count = n_z * cap
    return pl.pallas_call(
        functools.partial(partials_kernel, scale, n_z, cap, len(dy_pieces)),
        in_specs=[SMEM, SMEM] + [ANY] * len(dy_pieces) + [VMEM] * len(hidden_pieces),
        out_specs=VMEM,
        out_shape=shaped(jnp.bfloat16, count, block, block),
        scratch_shapes=[
            pltpu.VMEM((whole, width), jnp.bfloat16),
            pltpu.VMEM((rows, block, whole), jnp.bfloat16),
            pltpu.SemaphoreType.DMA((len(dy_pieces),)),
        ],
        cost_estimate=cost(
            2 * count * block * block * whole, 2 * whole * (width + rows * block)
        ),
        name="partial_blocks",
    )(ids, at, *dy_pieces, *hidden_pieces)


def grads_kernel(own_ref, left_ref, right_ref, top_ref, bottom_ref, act_ref, out_ref):
    row_count, tokens, block = own_ref.shape
    parts, _, rows, _ = act_ref.shape
    half = tokens // 2
    for r in range(row_count):
        span = slice(r * block, (r + 1) * block)
        for p in range(parts):
            here = slice(p * rows, (p + 1) * rows)
            low = p * rows < half
            across = top_ref if low else bottom_ref
            there = here if low else slice(p * rows - half, (p + 1) * rows - half)
            dh = (
                own_ref[r, here]
                + left_ref[r, here].astype(jnp.float32)
                + right_ref[r, here].astype(jnp.float32)
                + across[r, there].astype(jnp.float32)
            )
            dh = dh.astype(jnp.bfloat16).astype(jnp.float32)
            gate = act_ref[p, 0, :, span].astype(jnp.float32)
            up = act_ref[p, 1, :, span].astype(jnp.float32)
            sig = jax.nn.sigmoid(gate)
            out_ref[p, 0, :, span] = (dh * up * (sig * (1.0 + gate * (1.0 - sig)))).astype(
                jnp.bfloat16
            )
            out_ref[p, 1, :, span] = (dh * (gate * sig)).astype(jnp.bfloat16)


def activation_grads(own, left, right, top, bottom, act):
    return pl.pallas_call(
        grads_kernel,
        in_specs=[VMEM] * 6,
        out_specs=VMEM,
        out_shape=shaped(jnp.bfloat16, *act.shape),
        cost_estimate=cost(8 * act.size, 10 * own.size + 4 * act.size, act.size // 2),
        name="activation_grads",
    )(own, left, right, top, bottom, act)


def body(gate_pre, up_pre, cotangent, w_slots, slot_ids):
    n_fsdp = lax.axis_size("fsdp")
    n_tensor = lax.axis_size("tensor")
    n_x, n_z = X_CHIPS, n_fsdp // X_CHIPS
    cap, block = w_slots.shape[1], w_slots.shape[2]
    rows = gate_pre.shape[1] // n_tensor // block
    half = cotangent.shape[0] // 2
    together = lax.optimization_barrier

    def shift(value, x_by, z_by):
        pairs = [
            (x * n_z + z, (x + x_by) % n_x * n_z + (z + z_by) % n_z)
            for x in range(n_x)
            for z in range(n_z)
        ]
        return lax.ppermute(value, "fsdp", pairs)

    me = lax.axis_index("fsdp")
    at = jnp.stack([me // n_z, me % n_z]).astype(jnp.int32)
    ids = slot_ids[0]
    own = w_slots[0]

    z_groups = [[x * n_z + z for z in range(n_z)] for x in range(n_x)]
    weights = lax.all_gather(own, "fsdp", axis=0, tiled=True, axis_index_groups=z_groups)
    dy_right, dy_left = shift(cotangent, -1, 0), shift(cotangent, 1, 0)
    act = lax.all_to_all(
        pack(gate_pre, up_pre, n_tensor), "tensor", split_axis=0, concat_axis=0, tiled=True
    )
    hidden = hidden_of(act)
    h_right, h_left = shift(hidden, -1, 0), shift(hidden, 1, 0)
    dy_top, dy_bottom = shift(dy_right[:half], -1, 0), shift(dy_left[half:], 1, 0)
    h_top, h_bottom = shift(h_right[:half], -1, 0), shift(h_left[half:], 1, 0)

    scale = 1.0 / math.sqrt(cotangent.shape[0] * n_fsdp)
    dys = [cotangent, dy_right, dy_left, dy_top, dy_bottom]
    hiddens = [hidden, h_right, h_left, h_top, h_bottom]
    partials = partial_blocks(ids, at, dys, hiddens, block, n_z, cap, scale)
    partials, *dys = together((partials, *dys))
    w_grad = lax.psum_scatter(
        partials, "fsdp", scatter_dimension=0, tiled=True, axis_index_groups=z_groups
    ).astype(jnp.float32)[None]

    mine, to_right, to_left, top, bottom = block_products(ids, at, dys, weights, rows, n_z, cap)
    got_left, got_right = shift(to_right, 1, 0), shift(to_left, -1, 0)
    got_top, got_bottom = shift(top, 2, 0), shift(bottom, -2, 0)
    grads = activation_grads(mine, got_left, got_right, got_top, got_bottom, act)
    grads = lax.all_to_all(grads, "tensor", split_axis=0, concat_axis=0, tiled=True)
    d_gate, d_up = unpack(grads)
    return (d_gate, d_up, w_grad)


def solution(mesh):
    placed = (
        P(("fsdp", "tensor"), None),
        P(("fsdp", "tensor"), None),
        P("fsdp", None),
        P("tensor", "fsdp", None, None),
        P("tensor", None),
    )
    return jax.shard_map(
        body,
        mesh=mesh,
        in_specs=placed,
        out_specs=(
            P(("fsdp", "tensor"), None),
            P(("fsdp", "tensor"), None),
            P("tensor", "fsdp", None, None),
        ),
        check_vma=False,
    )
```

```python
import functools
import math

import jax
import jax.numpy as jnp
from jax import lax
from jax.experimental import pallas as pl
from jax.experimental.pallas import tpu as pltpu
from jax.sharding import PartitionSpec as P

X_CHIPS = 4
VMEM = pl.BlockSpec(memory_space=pltpu.VMEM)
SMEM = pl.BlockSpec(memory_space=pltpu.SMEM)
ANY = pl.BlockSpec(memory_space=pl.ANY)


def shaped(dtype, *shape):
    return jax.ShapeDtypeStruct(shape, dtype)


def cost(flops, moved, transcendentals=0):
    return pl.CostEstimate(flops=flops, bytes_accessed=moved, transcendentals=transcendentals)


def pack_kernel(gate_ref, up_ref, out_ref):
    cols = out_ref.shape[3]
    for p in range(out_ref.shape[0]):
        out_ref[p, 0] = gate_ref[:, p * cols : (p + 1) * cols]
        out_ref[p, 1] = up_ref[:, p * cols : (p + 1) * cols]


def pack(gate, up, parts):
    rows, width = gate.shape
    cols = width // parts
    steps = 2
    return pl.pallas_call(
        pack_kernel,
        grid=(steps,),
        in_specs=[pl.BlockSpec((rows, width // steps), lambda i: (0, i))] * 2,
        out_specs=pl.BlockSpec((parts // steps, 2, rows, cols), lambda i: (i, 0, 0, 0)),
        out_shape=shaped(gate.dtype, parts, 2, rows, cols),
        cost_estimate=cost(0, 8 * rows * width),
        name="pack",
    )(gate, up)


def unpack_kernel(in_ref, gate_ref, up_ref):
    cols = in_ref.shape[3]
    for p in range(in_ref.shape[0]):
        gate_ref[:, p * cols : (p + 1) * cols] = in_ref[p, 0]
        up_ref[:, p * cols : (p + 1) * cols] = in_ref[p, 1]


def unpack(packed):
    parts, _, rows, cols = packed.shape
    steps = 2
    shape = shaped(packed.dtype, rows, parts * cols)
    return pl.pallas_call(
        unpack_kernel,
        grid=(steps,),
        in_specs=[pl.BlockSpec((parts // steps, 2, rows, cols), lambda i: (i, 0, 0, 0))],
        out_specs=[pl.BlockSpec((rows, parts * cols // steps), lambda i: (0, i))] * 2,
        out_shape=[shape, shape],
        cost_estimate=cost(0, 8 * rows * parts * cols),
        name="unpack",
    )(packed)


def hidden_kernel(act_ref, out_ref):
    rows = act_ref.shape[2]
    for p in range(act_ref.shape[0]):
        gate = act_ref[p, 0].astype(jnp.float32)
        up = act_ref[p, 1].astype(jnp.float32)
        out_ref[p * rows : (p + 1) * rows, :] = (gate * jax.nn.sigmoid(gate) * up).astype(
            jnp.bfloat16
        )


def hidden_of(act):
    parts, _, rows, cols = act.shape
    return pl.pallas_call(
        hidden_kernel,
        in_specs=[VMEM],
        out_specs=VMEM,
        out_shape=shaped(jnp.bfloat16, parts * rows, cols),
        cost_estimate=cost(4 * act.size, 3 * act.size, act.size // 2),
        name="hidden",
    )(act)


def fetch(pieces, plan, core, whole, sem):
    copies = []
    for k, (source, source_at, rows, base, side) in enumerate(plan):
        to = base if side is None else base + rows * (core if side == 0 else 1 - core)
        copies.append(
            pltpu.make_async_copy(
                pieces[source].at[pl.ds(source_at, rows)], whole.at[pl.ds(to, rows)], sem.at[k]
            )
        )
    for copy in copies:
        copy.start()
    return copies


def place_of(slot, col_bits, block):
    safe = jnp.maximum(slot, 0)
    col = pl.multiple_of((safe & ((1 << col_bits) - 1)) * block, block)
    return safe >> col_bits, col


def products_kernel(n_z, cap, n_pieces, plan, spans, ids_ref, at_ref, *refs):
    dy_pieces = refs[:n_pieces]
    w_ref = refs[n_pieces]
    outs = refs[n_pieces + 1 : n_pieces + 1 + len(spans)]
    dy, total, sem = refs[n_pieces + 1 + len(spans) :]
    block = w_ref.shape[1]
    row_count = total.shape[0] - 1
    col_bits = (dy.shape[1] // block).bit_length() - 1
    copies = fetch(dy_pieces, plan, at_ref[2], dy, sem)
    total[...] = jnp.zeros_like(total)
    for copy in copies:
        copy.wait()
    start = at_ref[0] * n_z * cap

    def advance(i, carry):
        rows, products = [], []
        for j in range(cap):
            slot = ids_ref[start + i * cap + j]
            row, col = place_of(slot, col_bits, block)
            rows.append(jnp.where(slot >= 0, row, row_count))
            products.append(
                lax.dot_general(
                    dy[:, pl.ds(col, block)],
                    w_ref[i * cap + j],
                    (((1,), (1,)), ((), ())),
                    preferred_element_type=jnp.float32,
                )
            )
        for row, product in zip(rows, products):
            total[row] += product
        return carry

    lax.fori_loop(0, n_z, advance, 0)
    for r in range(row_count):
        for out, (at, rows, _) in zip(outs, spans):
            out[r] = total[r, at : at + rows].astype(out.dtype)


def block_products(ids, at, dy_pieces, plan, weights, spans, rows, n_z, cap):
    width = dy_pieces[0].shape[1]
    block = weights.shape[1]
    whole = sum(span[1] for span in spans)
    return pl.pallas_call(
        functools.partial(products_kernel, n_z, cap, len(dy_pieces), plan, spans),
        in_specs=[SMEM, SMEM] + [ANY] * len(dy_pieces) + [VMEM],
        out_specs=[VMEM] * len(spans),
        out_shape=[shaped(dtype, rows, n, block) for _, n, dtype in spans],
        scratch_shapes=[
            pltpu.VMEM((whole, width), jnp.bfloat16),
            pltpu.VMEM((rows + 1, whole, block), jnp.float32),
            pltpu.SemaphoreType.DMA((len(plan),)),
        ],
        cost_estimate=cost(
            2 * weights.size * whole, 2 * whole * width + 2 * weights.size + 4 * rows * whole * block
        ),
        name="block_products",
    )(ids, at, *dy_pieces, weights)


def partials_kernel(scale, n_z, cap, n_pieces, plan, hidden_at, last, ids_ref, at_ref, *refs):
    dy_pieces = refs[:n_pieces]
    hidden_pieces = refs[n_pieces : n_pieces + len(hidden_at)]
    rest = refs[n_pieces + len(hidden_at) :]
    if last:
        given_ref, out_ref, dy, hidden_t, sem = rest
    else:
        out_ref, dy, hidden_t, sem = rest
    row_count, block, _ = hidden_t.shape
    col_bits = (dy.shape[1] // block).bit_length() - 1
    copies = fetch(dy_pieces, plan, at_ref[2], dy, sem)
    for piece, at in zip(hidden_pieces, hidden_at):
        tokens = piece.shape[0]
        for r in range(row_count):
            value = piece[:, r * block : (r + 1) * block].astype(jnp.float32)
            hidden_t[r, :, at : at + tokens] = value.T.astype(jnp.bfloat16)
    for copy in copies:
        copy.wait()
    start = at_ref[0] * n_z * cap
    group = 2 * cap

    def advance(i, carry):
        for j in range(group):
            slot = ids_ref[start + i * group + j]
            row, col = place_of(slot, col_bits, block)
            value = jnp.dot(
                hidden_t[row], dy[:, pl.ds(col, block)], preferred_element_type=jnp.float32
            )
            if last:
                factor = jnp.where(slot >= 0, jnp.float32(scale), jnp.float32(0))
                value = (value + given_ref[i * group + j]) * factor
            out_ref[i * group + j] = value.astype(out_ref.dtype)
        return carry

    lax.fori_loop(0, n_z // 2, advance, 0)


def partial_blocks(ids, at, dy_pieces, plan, hidden_pieces, block, n_z, cap, scale, given=None):
    last = given is not None
    width = dy_pieces[0].shape[1]
    hidden_at, whole = [], 0
    for piece in hidden_pieces:
        hidden_at.append(whole)
        whole += piece.shape[0]
    rows = hidden_pieces[0].shape[1] // block
    count = n_z * cap
    n_pieces = len(dy_pieces)
    return pl.pallas_call(
        functools.partial(
            partials_kernel, scale, n_z, cap, n_pieces, plan, tuple(hidden_at), last
        ),
        in_specs=[SMEM, SMEM]
        + [ANY] * n_pieces
        + [VMEM] * (len(hidden_pieces) + last),
        out_specs=VMEM,
        out_shape=shaped(jnp.bfloat16 if last else jnp.float32, count, block, block),
        scratch_shapes=[
            pltpu.VMEM((whole, width), jnp.bfloat16),
            pltpu.VMEM((rows, block, whole), jnp.bfloat16),
            pltpu.SemaphoreType.DMA((len(plan),)),
        ],
        cost_estimate=cost(
            2 * count * block * block * whole,
            2 * whole * (width + rows * block) + 6 * count * block * block,
        ),
        name="partial_blocks",
    )(ids, at, *dy_pieces, *hidden_pieces, *([given] if last else []))


def grads_kernel(own_ref, left_ref, right_ref, top_ref, bottom_ref, act_ref, out_ref):
    row_count, tokens, block = own_ref.shape
    parts, _, rows, _ = act_ref.shape
    half = tokens // 2
    for r in range(row_count):
        span = slice(r * block, (r + 1) * block)
        for p in range(parts):
            here = slice(p * rows, (p + 1) * rows)
            low = p * rows < half
            across = top_ref if low else bottom_ref
            there = here if low else slice(p * rows - half, (p + 1) * rows - half)
            dh = (
                own_ref[r, here]
                + left_ref[r, here].astype(jnp.float32)
                + right_ref[r, here].astype(jnp.float32)
                + across[r, there].astype(jnp.float32)
            )
            dh = dh.astype(jnp.bfloat16).astype(jnp.float32)
            gate = act_ref[p, 0, :, span].astype(jnp.float32)
            up = act_ref[p, 1, :, span].astype(jnp.float32)
            sig = jax.nn.sigmoid(gate)
            out_ref[p, 0, :, span] = (dh * up * (sig * (1.0 + gate * (1.0 - sig)))).astype(
                jnp.bfloat16
            )
            out_ref[p, 1, :, span] = (dh * (gate * sig)).astype(jnp.bfloat16)


def activation_grads(own, left, right, top, bottom, act):
    return pl.pallas_call(
        grads_kernel,
        in_specs=[VMEM] * 6,
        out_specs=VMEM,
        out_shape=shaped(jnp.bfloat16, *act.shape),
        cost_estimate=cost(8 * act.size, 10 * own.size + 4 * act.size, act.size // 2),
        name="activation_grads",
    )(own, left, right, top, bottom, act)


def body(gate_pre, up_pre, cotangent, w_slots, slot_ids):
    n_fsdp = lax.axis_size("fsdp")
    n_tensor = lax.axis_size("tensor")
    n_x, n_z = X_CHIPS, n_fsdp // X_CHIPS
    cap, block = w_slots.shape[1], w_slots.shape[2]
    rows = gate_pre.shape[1] // n_tensor // block
    tokens = cotangent.shape[0]
    half = tokens // 2
    together = lax.optimization_barrier

    def shift(value, x_by, z_by):
        pairs = [
            (x * n_z + z, (x + x_by) % n_x * n_z + (z + z_by) % n_z)
            for x in range(n_x)
            for z in range(n_z)
        ]
        return lax.ppermute(value, "fsdp", pairs)

    def swap(value):
        return lax.ppermute(value, "tensor", [(t, t ^ 1) for t in range(n_tensor)])

    me = lax.axis_index("fsdp")
    core = lax.axis_index("tensor") % 2
    at = jnp.stack([me // n_z, me % n_z, core]).astype(jnp.int32)
    ids = slot_ids[0]
    own = w_slots[0]

    z_groups = [[x * n_z + z for z in range(n_z)] for x in range(n_x)]
    weights = lax.all_gather(own, "fsdp", axis=0, tiled=True, axis_index_groups=z_groups)
    packed = pack(gate_pre, up_pre, n_tensor)
    packed, share = together((packed, lax.dynamic_slice_in_dim(cotangent, core * half, half)))
    act = lax.all_to_all(packed, "tensor", split_axis=0, concat_axis=0, tiled=True)
    dy_right, dy_left = shift(share, -1, 0), shift(share, 1, 0)
    hidden = hidden_of(act)
    hidden, dy_right, dy_left = together((hidden, dy_right, dy_left))
    h_right, h_left = shift(hidden, -1, 0), shift(hidden, 1, 0)
    dy_top = shift(dy_right[: half // 2], -1, 0)
    dy_bottom = shift(dy_left[half // 2 :], 1, 0)
    near = jnp.concatenate([dy_right, dy_left])
    near_swap = swap(near)
    far = jnp.concatenate([dy_top, dy_bottom])
    far_swap = swap(far)
    h_top, h_bottom = shift(h_right[:half], -1, 0), shift(h_left[half:], 1, 0)

    def near_plan(base, first):
        return tuple(
            (first + side, source_at, half, base + offset, side)
            for side in (0, 1)
            for source_at, offset in ((0, 0), (half, tokens))
        )

    scale = 1.0 / math.sqrt(tokens * n_fsdp)
    own_plan = ((0, 0, tokens, 0, None),)
    far_plan = ((0, 0, half, 0, 0), (1, 0, half, 0, 1))
    partials = partial_blocks(
        ids,
        at,
        [cotangent, near, near_swap],
        own_plan + near_plan(tokens, 1),
        [hidden, h_right, h_left],
        block,
        n_z,
        cap,
        scale,
    )
    partials = partial_blocks(
        ids, at, [far, far_swap], far_plan, [h_top, h_bottom], block, n_z, cap, scale, partials
    )
    partials, near, near_swap = together((partials, near, near_swap))
    w_grad = lax.psum_scatter(
        partials, "fsdp", scatter_dimension=0, tiled=True, axis_index_groups=z_groups
    ).astype(jnp.float32)[None]

    def products(pieces, plan, spans):
        return block_products(ids, at, pieces, plan, weights, spans, rows, n_z, cap)

    narrow = jnp.bfloat16
    to_right, to_left = products(
        [near, near_swap], near_plan(0, 0), ((0, tokens, narrow), (tokens, tokens, narrow))
    )
    got_left, got_right = shift(to_right, 1, 0), shift(to_left, -1, 0)
    far, far_swap, to_right = together((far, far_swap, to_right))
    top, bottom = products([far, far_swap], far_plan, ((0, half, narrow), (half, half, narrow)))
    got_top, got_bottom = shift(top, 2, 0), shift(bottom, -2, 0)
    mine_dy, top = together((cotangent, top))
    (mine,) = products([mine_dy], own_plan, ((0, tokens, jnp.float32),))
    grads = activation_grads(mine, got_left, got_right, got_top, got_bottom, act)
    grads = lax.all_to_all(grads, "tensor", split_axis=0, concat_axis=0, tiled=True)
    d_gate, d_up = unpack(grads)
    return (d_gate, d_up, w_grad)


def solution(mesh):
    placed = (
        P(("fsdp", "tensor"), None),
        P(("fsdp", "tensor"), None),
        P("fsdp", None),
        P("tensor", "fsdp", None, None),
        P("tensor", None),
    )
    return jax.shard_map(
        body,
        mesh=mesh,
        in_specs=placed,
        out_specs=(
            P(("fsdp", "tensor"), None),
            P(("fsdp", "tensor"), None),
            P("tensor", "fsdp", None, None),
        ),
        check_vma=False,
    )
```

```python
import functools
import math

import jax
import jax.numpy as jnp
from jax import lax
from jax.experimental import pallas as pl
from jax.experimental.pallas import tpu as pltpu
from jax.sharding import PartitionSpec as P


X_CHIPS = 4
B_OWNERS = 4
P_OWNERS = 8
VMEM = pl.BlockSpec(memory_space=pltpu.VMEM)
SMEM = pl.BlockSpec(memory_space=pltpu.SMEM)
ANY = pl.BlockSpec(memory_space=pl.ANY)


def shaped(dtype, *shape):
    return jax.ShapeDtypeStruct(shape, dtype)


def cost(flops, moved, transcendentals=0):
    return pl.CostEstimate(flops=flops, bytes_accessed=moved, transcendentals=transcendentals)


def pack_kernel(gate_ref, up_ref, out_ref):
    cols = out_ref.shape[3]
    for p in range(out_ref.shape[0]):
        out_ref[p, 0] = gate_ref[:, p * cols : (p + 1) * cols]
        out_ref[p, 1] = up_ref[:, p * cols : (p + 1) * cols]


def pack(gate, up, parts):
    rows, width = gate.shape
    cols = width // parts
    steps = 2
    return pl.pallas_call(
        pack_kernel,
        grid=(steps,),
        in_specs=[pl.BlockSpec((rows, width // steps), lambda i: (0, i))] * 2,
        out_specs=pl.BlockSpec((parts // steps, 2, rows, cols), lambda i: (i, 0, 0, 0)),
        out_shape=shaped(gate.dtype, parts, 2, rows, cols),
        cost_estimate=cost(0, 8 * rows * width),
        name="pack",
    )(gate, up)


def unpack_kernel(in_ref, gate_ref, up_ref):
    cols = in_ref.shape[3]
    for p in range(in_ref.shape[0]):
        gate_ref[:, p * cols : (p + 1) * cols] = in_ref[p, 0]
        up_ref[:, p * cols : (p + 1) * cols] = in_ref[p, 1]


def unpack(packed):
    parts, _, rows, cols = packed.shape
    steps = 2
    shape = shaped(packed.dtype, rows, parts * cols)
    return pl.pallas_call(
        unpack_kernel,
        grid=(steps,),
        in_specs=[pl.BlockSpec((parts // steps, 2, rows, cols), lambda i: (i, 0, 0, 0))],
        out_specs=[pl.BlockSpec((rows, parts * cols // steps), lambda i: (0, i))] * 2,
        out_shape=[shape, shape],
        cost_estimate=cost(0, 8 * rows * parts * cols),
        name="unpack",
    )(packed)


def hidden_kernel(act_ref, out_ref):
    rows = act_ref.shape[2]
    for p in range(act_ref.shape[0]):
        gate = act_ref[p, 0].astype(jnp.float32)
        up = act_ref[p, 1].astype(jnp.float32)
        out_ref[p * rows : (p + 1) * rows, :] = (gate * jax.nn.sigmoid(gate) * up).astype(
            jnp.bfloat16
        )


def hidden_of(act):
    parts, _, rows, cols = act.shape
    return pl.pallas_call(
        hidden_kernel,
        in_specs=[VMEM],
        out_specs=VMEM,
        out_shape=shaped(jnp.bfloat16, parts * rows, cols),
        cost_estimate=cost(4 * act.size, 3 * act.size, act.size // 2),
        name="hidden",
    )(act)


def fetch(pieces, plan, core, whole, sem):
    copies = []
    for k, (source, source_at, rows, base, side) in enumerate(plan):
        to = base if side is None else base + rows * (core if side == 0 else 1 - core)
        copies.append(
            pltpu.make_async_copy(
                pieces[source].at[pl.ds(source_at, rows)], whole.at[pl.ds(to, rows)], sem.at[k]
            )
        )
    for copy in copies:
        copy.start()
    return copies


def place_of(slot, col_bits, block):
    safe = jnp.maximum(slot, 0)
    col = pl.multiple_of((safe & ((1 << col_bits) - 1)) * block, block)
    return safe >> col_bits, col


def products_kernel(n_z, cap, n_pieces, plan, spans, ids_ref, at_ref, *refs):
    dy_pieces = refs[:n_pieces]
    w_ref = refs[n_pieces]
    outs = refs[n_pieces + 1 : n_pieces + 1 + len(spans)]
    dy, total, sem = refs[n_pieces + 1 + len(spans) :]
    block = w_ref.shape[1]
    row_count = total.shape[0] - 1
    col_bits = (dy.shape[1] // block).bit_length() - 1
    copies = fetch(dy_pieces, plan, at_ref[2], dy, sem)
    total[...] = jnp.zeros_like(total)
    for copy in copies:
        copy.wait()
    start = at_ref[0] * n_z * cap

    def advance(i, carry):
        rows, products = [], []
        for j in range(B_OWNERS * cap):
            slot = ids_ref[start + i * B_OWNERS * cap + j]
            row, col = place_of(slot, col_bits, block)
            rows.append(jnp.where(slot >= 0, row, row_count))
            products.append(
                lax.dot_general(
                    dy[:, pl.ds(col, block)],
                    w_ref[i * B_OWNERS * cap + j],
                    (((1,), (1,)), ((), ())),
                    preferred_element_type=jnp.float32,
                )
            )
        for row, product in zip(rows, products):
            total[row] += product
        return carry

    lax.fori_loop(0, n_z // B_OWNERS, advance, 0)
    for r in range(row_count):
        for out, (at, rows, _) in zip(outs, spans):
            out[r] = total[r, at : at + rows].astype(out.dtype)


def block_products(ids, at, dy_pieces, plan, weights, spans, rows, n_z, cap):
    width = dy_pieces[0].shape[1]
    block = weights.shape[1]
    whole = sum(span[1] for span in spans)
    return pl.pallas_call(
        functools.partial(products_kernel, n_z, cap, len(dy_pieces), plan, spans),
        in_specs=[SMEM, SMEM] + [ANY] * len(dy_pieces) + [VMEM],
        out_specs=[VMEM] * len(spans),
        out_shape=[shaped(dtype, rows, n, block) for _, n, dtype in spans],
        scratch_shapes=[
            pltpu.VMEM((whole, width), jnp.bfloat16),
            pltpu.VMEM((rows + 1, whole, block), jnp.float32),
            pltpu.SemaphoreType.DMA((len(plan),)),
        ],
        cost_estimate=cost(
            2 * weights.size * whole, 2 * whole * width + 2 * weights.size + 4 * rows * whole * block
        ),
        name="block_products",
    )(ids, at, *dy_pieces, weights)


def partials_kernel(scale, n_z, cap, n_pieces, plan, hidden_at, last, ids_ref, at_ref, *refs):
    dy_pieces = refs[:n_pieces]
    hidden_pieces = refs[n_pieces : n_pieces + len(hidden_at)]
    rest = refs[n_pieces + len(hidden_at) :]
    if last:
        given_ref, out_ref, dy, hidden_t, sem = rest
    else:
        out_ref, dy, hidden_t, sem = rest
    row_count, block, _ = hidden_t.shape
    col_bits = (dy.shape[1] // block).bit_length() - 1
    copies = fetch(dy_pieces, plan, at_ref[2], dy, sem)
    for piece, at in zip(hidden_pieces, hidden_at):
        tokens = piece.shape[0]
        for r in range(row_count):
            value = piece[:, r * block : (r + 1) * block].astype(jnp.float32)
            hidden_t[r, :, at : at + tokens] = value.T.astype(jnp.bfloat16)
    for copy in copies:
        copy.wait()
    start = at_ref[0] * n_z * cap
    group = P_OWNERS * cap

    def advance(i, carry):
        for j in range(group):
            slot = ids_ref[start + i * group + j]
            row, col = place_of(slot, col_bits, block)
            value = jnp.dot(
                hidden_t[row], dy[:, pl.ds(col, block)], preferred_element_type=jnp.float32
            )
            if last:
                factor = jnp.where(slot >= 0, jnp.float32(scale), jnp.float32(0))
                value = (value + given_ref[i * group + j]) * factor
            out_ref[i * group + j] = value.astype(out_ref.dtype)
        return carry

    lax.fori_loop(0, n_z // P_OWNERS, advance, 0)


def partial_blocks(ids, at, dy_pieces, plan, hidden_pieces, block, n_z, cap, scale, given=None):
    last = given is not None
    width = dy_pieces[0].shape[1]
    hidden_at, whole = [], 0
    for piece in hidden_pieces:
        hidden_at.append(whole)
        whole += piece.shape[0]
    rows = hidden_pieces[0].shape[1] // block
    count = n_z * cap
    n_pieces = len(dy_pieces)
    return pl.pallas_call(
        functools.partial(
            partials_kernel, scale, n_z, cap, n_pieces, plan, tuple(hidden_at), last
        ),
        in_specs=[SMEM, SMEM]
        + [ANY] * n_pieces
        + [VMEM] * (len(hidden_pieces) + last),
        out_specs=VMEM,
        out_shape=shaped(jnp.bfloat16 if last else jnp.float32, count, block, block),
        scratch_shapes=[
            pltpu.VMEM((whole, width), jnp.bfloat16),
            pltpu.VMEM((rows, block, whole), jnp.bfloat16),
            pltpu.SemaphoreType.DMA((len(plan),)),
        ],
        cost_estimate=cost(
            2 * count * block * block * whole,
            2 * whole * (width + rows * block) + 6 * count * block * block,
        ),
        name="partial_blocks",
    )(ids, at, *dy_pieces, *hidden_pieces, *([given] if last else []))


def grads_kernel(own_ref, left_ref, right_ref, far_ref, act_ref, out_ref):
    row_count, _, block = own_ref.shape
    parts, _, rows, _ = act_ref.shape
    for r in range(row_count):
        span = slice(r * block, (r + 1) * block)
        for p in range(parts):
            here = slice(p * rows, (p + 1) * rows)
            dh = (
                own_ref[r, here]
                + left_ref[r, here].astype(jnp.float32)
                + right_ref[r, here].astype(jnp.float32)
                + far_ref[r, here].astype(jnp.float32)
            )
            dh = dh.astype(jnp.bfloat16).astype(jnp.float32)
            gate = act_ref[p, 0, :, span].astype(jnp.float32)
            up = act_ref[p, 1, :, span].astype(jnp.float32)
            sig = jax.nn.sigmoid(gate)
            out_ref[p, 0, :, span] = (dh * up * (sig * (1.0 + gate * (1.0 - sig)))).astype(
                jnp.bfloat16
            )
            out_ref[p, 1, :, span] = (dh * (gate * sig)).astype(jnp.bfloat16)


def activation_grads(own, left, right, far, act):
    return pl.pallas_call(
        grads_kernel,
        in_specs=[VMEM] * 5,
        out_specs=VMEM,
        out_shape=shaped(jnp.bfloat16, *act.shape),
        cost_estimate=cost(8 * act.size, 10 * own.size + 4 * act.size, act.size // 2),
        name="activation_grads",
    )(own, left, right, far, act)


def body(gate_pre, up_pre, cotangent, w_slots, slot_ids):
    n_fsdp = lax.axis_size("fsdp")
    n_tensor = lax.axis_size("tensor")
    n_x, n_z = X_CHIPS, n_fsdp // X_CHIPS
    cap, block = w_slots.shape[1], w_slots.shape[2]
    rows = gate_pre.shape[1] // n_tensor // block
    tokens = cotangent.shape[0]
    half = tokens // 2
    together = lax.optimization_barrier

    def shift(value, x_by, z_by):
        pairs = [
            (x * n_z + z, (x + x_by) % n_x * n_z + (z + z_by) % n_z)
            for x in range(n_x)
            for z in range(n_z)
        ]
        return lax.ppermute(value, "fsdp", pairs)

    def swap(value):
        return lax.ppermute(value, "tensor", [(t, t ^ 1) for t in range(n_tensor)])

    me = lax.axis_index("fsdp")
    core = lax.axis_index("tensor") % 2
    at = jnp.stack([me // n_z, me % n_z, core]).astype(jnp.int32)
    ids = slot_ids[0]
    own = w_slots[0]

    z_groups = [[x * n_z + z for z in range(n_z)] for x in range(n_x)]
    weights = lax.all_gather(own, "fsdp", axis=0, tiled=True, axis_index_groups=z_groups)
    packed = pack(gate_pre, up_pre, n_tensor)
    packed, share = together((packed, lax.dynamic_slice_in_dim(cotangent, core * half, half)))
    act = lax.all_to_all(packed, "tensor", split_axis=0, concat_axis=0, tiled=True)
    dy_right, dy_left, dy_far = shift(share, -1, 0), shift(share, 1, 0), shift(share, 2, 0)
    hidden = hidden_of(act)
    h_right, h_left, h_far = shift(hidden, -1, 0), shift(hidden, 1, 0), shift(hidden, 2, 0)
    hidden, dy_right, dy_left = together((hidden, dy_right, dy_left))
    near = [dy_right, swap(dy_right), dy_left, swap(dy_left)]
    far = [dy_far, swap(dy_far)]

    def plan_of(first, count, base):
        return tuple(
            (first + k, 0, half, base + k // 2 * tokens, k % 2) for k in range(count)
        )

    scale = 1.0 / math.sqrt(tokens * n_fsdp)
    own_plan = ((0, 0, tokens, 0, None),)
    partials = partial_blocks(
        ids,
        at,
        [cotangent, *near],
        own_plan + plan_of(1, 4, tokens),
        [hidden, h_right, h_left],
        block,
        n_z,
        cap,
        scale,
    )
    partials = partial_blocks(
        ids, at, far, plan_of(0, 2, 0), [h_far], block, n_z, cap, scale, partials
    )
    partials, *near = together((partials, *near))
    w_grad = lax.psum_scatter(
        partials, "fsdp", scatter_dimension=0, tiled=True, axis_index_groups=z_groups
    )

    def products(pieces, plan, spans):
        return block_products(ids, at, pieces, plan, weights, spans, rows, n_z, cap)

    narrow = jnp.bfloat16
    to_right, to_left = products(
        near, plan_of(0, 4, 0), ((0, tokens, narrow), (tokens, tokens, narrow))
    )
    got_left, got_right = shift(to_right, 1, 0), shift(to_left, -1, 0)
    *far, to_right = together((*far, to_right))
    (to_far,) = products(far, plan_of(0, 2, 0), ((0, tokens, narrow),))
    got_far = shift(to_far, 2, 0)
    mine_dy, to_far = together((cotangent, to_far))
    (mine,) = products([mine_dy], own_plan, ((0, tokens, jnp.float32),))
    grads = activation_grads(mine, got_left, got_right, got_far, act)
    grads = lax.all_to_all(grads, "tensor", split_axis=0, concat_axis=0, tiled=True)
    d_gate, d_up = unpack(grads)
    d_gate, d_up, w_grad = together((d_gate, d_up, w_grad))
    w_grad = w_grad.astype(jnp.float32)[None]
    return (d_gate, d_up, w_grad)


def solution(mesh):
    placed = (
        P(("fsdp", "tensor"), None),
        P(("fsdp", "tensor"), None),
        P("fsdp", None),
        P("tensor", "fsdp", None, None),
        P("tensor", None),
    )
    return jax.shard_map(
        body,
        mesh=mesh,
        in_specs=placed,
        out_specs=(
            P(("fsdp", "tensor"), None),
            P(("fsdp", "tensor"), None),
            P("tensor", "fsdp", None, None),
        ),
        check_vma=False,
    )
```
